768 devices in a mesh: replica: 48 (over z, y_hi), fsdp: 16 (over x, y_lo, core).
Axes of the slice: x: 4, y: 8 (y_hi: 4, y_lo: 2; y = y_hi * 2 + y_lo), z: 12, core: 2. Of those that a mesh axis runs over, the one named last changes fastest.
Arguments:
- activations: bfloat16 [48, 2048, 8192], P('replica', 'fsdp'), may hold values from -6 to 6
- grad_out: bfloat16 [48, 2048, 1024], P('replica', 'fsdp'), may hold values from -6 to 6
- local_weight: bfloat16 [48, 8192, 1024], P('replica', 'fsdp'), may hold values from -6 to 6
- anchor: float32 [8192, 1024], P('fsdp'), may hold values from -6 to 6
- momentum: float32 [8192, 256], P('fsdp'), may hold values from -6 to 6
- projection_key: int32 [2], replicated, may hold values from 0 to 1073741823
Outputs:
- new_anchor: float32 [8192, 1024], P('fsdp')
- new_momentum: float32 [8192, 256], P('fsdp')
The draws below stay inside these ranges and needn't reach their ends.
All inputs are finite; a program needn't handle non-finite values.
Results may differ from the reference program's by a relative error of at most 0.0017.
Values may be sent and summed in bfloat16 or wider, within the bound.
No kernel may reach another device: no remote copies, remote signals or barrier semaphores. Data moves between devices by JAX's collectives and lax.ppermute only.
A program may use at most 32 MiB of HBM per device.

```python
import jax
import jax.numpy as jnp
from jax import lax

D = 8192
K = 1024
RANK = 256
TOK_REP = 2048
REPLICAS = 48


def steps_of(rng, dims, cuts, smallest, top_value):
    def one(position, shards_of):
        heights = jax.random.uniform(jax.random.fold_in(jax.random.fold_in(rng, 6), position), (shards_of,), jnp.float32, smallest / len(cuts), top_value / len(cuts))
        return jnp.repeat(jnp.exp(heights), dims[position] // shards_of).reshape((-1,) + (1,) * (len(dims) - position - 1))

    loudness = one(*cuts[0])
    for cut in cuts[1:]:
        loudness = loudness * one(*cut)
    return loudness


def centred(own_key, shape, deviation, reach, shards=(), dtype=jnp.bfloat16):
    level = steps_of(own_key, shape, shards, -0.22, 0.18) if shards else 1.0
    values = jax.random.normal(own_key, shape, jnp.float32) * deviation * level
    return jnp.minimum(jnp.maximum(values, -reach), reach).astype(dtype)


def setup_inputs(seed: int = 0) -> dict:
    seeds = jax.random.split(jax.random.key(seed), 7)
    activations = centred(seeds[0], (REPLICAS, TOK_REP, D), 1.0, 6.0, ((0, 48), (1, 16)))
    grad_out = centred(seeds[1], (REPLICAS, TOK_REP, K), 1.0, 6.0, ((0, 48), (1, 16)))
    local_weight = centred(seeds[2], (REPLICAS, D, K), 1.0, 6.0, ((0, 48), (1, 16)))
    anchor = centred(seeds[3], (D, K), 1.0, 6.0, ((0, 16),), jnp.float32)
    momentum = centred(seeds[4], (D, RANK), 1.0, 6.0, ((0, 16),), jnp.float32)
    projection_key = jax.random.randint(seeds[5], (2,), 0, 1073741824).astype(jnp.int32)
    return {"activations": activations, "grad_out": grad_out, "local_weight": local_weight, "anchor": anchor, "momentum": momentum, "projection_key": projection_key}


HIGH = lax.Precision.HIGHEST


def projection(words, rows, cols):
    k_index = lax.broadcasted_iota(jnp.int32, (rows, cols), 0)
    r_index = lax.broadcasted_iota(jnp.int32, (rows, cols), 1)
    hashed = words[0] + k_index * 668265261 + r_index * 374761393 + words[1] * 1103515245
    hashed = jnp.bitwise_xor(hashed, lax.shift_right_logical(hashed, jnp.int32(15)))
    hashed = hashed * 739982445
    hashed = jnp.bitwise_xor(hashed, lax.shift_right_logical(hashed, jnp.int32(12)))
    hashed = hashed * 695938361
    hashed = jnp.bitwise_xor(hashed, lax.shift_right_logical(hashed, jnp.int32(15)))
    level = jnp.bitwise_and(lax.shift_right_logical(hashed, jnp.int32(8)), 65535).astype(jnp.float32)
    return ((level + 0.5) / 65536.0 - 0.5) * (12.0 / rows_rank(cols)) ** 0.5


def rows_rank(cols):
    return float(cols)


def reference(activations, grad_out, local_weight, anchor, momentum, projection_key):
    proj = projection(projection_key, K, RANK)
    scale = float(TOK_REP) ** -0.5
    local_total = jnp.sum(local_weight.astype(jnp.float32), axis=0)
    drift_total = REPLICAS * anchor - local_total

    def one_replica(carry, pair):
        inputs, grads = pair
        projected = jnp.dot(grads.astype(jnp.float32), proj, precision=HIGH)
        part = jnp.dot(inputs.astype(jnp.float32).T, projected, precision=HIGH)
        return carry + part, None

    start = jnp.zeros((D, RANK), jnp.float32)
    grad_total, unused = lax.scan(one_replica, start, (activations, grad_out))
    summed = jnp.dot(drift_total, proj, precision=HIGH) + scale * grad_total
    compressed_mean = summed / REPLICAS
    new_momentum = 0.9 * momentum + compressed_mean
    update = compressed_mean + 0.9 * new_momentum
    new_anchor = anchor - 0.7 * jnp.dot(update, proj.T, precision=HIGH)
    return new_anchor, new_momentum
```

```python
import jax
import jax.numpy as jnp
from jax import lax
from jax.sharding import PartitionSpec as P

F32 = jnp.float32
BF16 = jnp.bfloat16


def projection_parts(words, rows, cols):
    k_index = lax.broadcasted_iota(jnp.int32, (rows, cols), 0)
    r_index = lax.broadcasted_iota(jnp.int32, (rows, cols), 1)
    hashed = words[0] + k_index * 668265261 + r_index * 374761393 + words[1] * 1103515245
    hashed = jnp.bitwise_xor(hashed, lax.shift_right_logical(hashed, jnp.int32(15)))
    hashed = hashed * 739982445
    hashed = jnp.bitwise_xor(hashed, lax.shift_right_logical(hashed, jnp.int32(12)))
    hashed = hashed * 695938361
    hashed = jnp.bitwise_xor(hashed, lax.shift_right_logical(hashed, jnp.int32(15)))
    high = jnp.bitwise_and(lax.shift_right_logical(hashed, jnp.int32(16)), 255).astype(F32)
    low = jnp.bitwise_and(lax.shift_right_logical(hashed, jnp.int32(8)), 255).astype(F32)
    return ((high - 127.5) * 256.0).astype(BF16), (low - 127.5).astype(BF16)


def halves(x):
    top = lax.reduce_precision(x, 8, 7)
    return top.astype(BF16), (x - top).astype(BF16)


def mm(a, b, dims=(((1,), (0,)), ((), ()))):
    return lax.dot_general(a, b, dims, preferred_element_type=F32)


def groups(z_of, y_of):
    return [[z * 4 + y for z in zs for y in ys] for zs in z_of for ys in y_of]


def on_device(activations, grad_out, local_weight, anchor, momentum, projection_key):
    inputs, grads, local = activations[0], grad_out[0], local_weight[0]
    tokens, width = inputs.shape
    width_k, rank = grads.shape[1], momentum.shape[1]
    rows = anchor.shape[0]
    replicas, shards = lax.axis_size("replica"), lax.axis_size("fsdp")
    unit = (12.0 / float(rank)) ** 0.5 / 65536.0
    scale = float(tokens * shards) ** (-0.5)
    chips = shards // 2
    core = lax.rem(lax.axis_index("fsdp"), 2)
    swap = [(i, i ^ 1) for i in range(shards)]
    same_core = [[2 * i + c for i in range(chips)] for c in range(2)]
    near = groups([range(4 * h, 4 * h + 4) for h in range(3)], [range(4)])
    far = groups([range(l, 12, 4) for l in range(4)], [[y] for y in range(4)])

    by_core = inputs.reshape(tokens, chips, 2, rows)
    keep = lax.dynamic_index_in_dim(by_core, core, 2, keepdims=False)
    give = lax.dynamic_index_in_dim(by_core, 1 - core, 2, keepdims=False)
    got = lax.ppermute(give, "fsdp", swap)
    got_grads = lax.ppermute(grads, "fsdp", swap)

    part_a, part_b = projection_parts(projection_key, width_k, rank)
    part_a, part_b = lax.optimization_barrier((part_a, part_b))

    def chip_half(acts, gs):
        projected = unit * (mm(gs, part_a) + mm(gs, part_b))
        top, rest = halves(projected)
        cols = acts.reshape(tokens, chips * rows)
        dims = (((0,), (0,)), ((), ()))
        return mm(cols, top, dims) + mm(cols, rest, dims)

    partial = (chip_half(keep, grads) + chip_half(got, got_grads)).astype(BF16)
    landed = lax.all_to_all(partial.reshape(chips, rows, rank), "fsdp", 0, 0, tiled=True, axis_index_groups=same_core)
    local_term = unit * (mm(local, part_a) + mm(local, part_b))
    mine = scale * jnp.sum(landed.astype(F32), axis=0) - local_term

    pieces = lax.all_to_all(mine.reshape(16, rows // 16, rank), "replica", 0, 0, tiled=True, axis_index_groups=near)
    piece = jnp.sum(pieces, axis=0)
    thirds = lax.all_to_all(jnp.broadcast_to(piece[None], (3,) + piece.shape), "replica", 0, 0, tiled=True, axis_index_groups=far)
    piece = jnp.sum(thirds, axis=0)
    spread = lax.all_to_all(jnp.broadcast_to(piece[None], (16,) + piece.shape), "replica", 0, 0, tiled=True, axis_index_groups=near)

    top, rest = halves(anchor)
    anchor_term = unit * (mm(top, part_a) + mm(top, part_b) + mm(rest, part_a))
    compressed_mean = anchor_term + spread.reshape(rows, rank) / replicas
    new_momentum = 0.9 * momentum + compressed_mean
    update = compressed_mean + 0.9 * new_momentum
    top, rest = halves(update)
    dims = (((1,), (1,)), ((), ()))
    product = mm(top, part_a, dims) + mm(top, part_b, dims) + mm(rest, part_a, dims)
    new_anchor = anchor - (0.7 * unit) * product
    return (new_anchor, new_momentum)


def solution(mesh):
    placed = (
        P("replica", "fsdp", None),
        P("replica", "fsdp", None),
        P("replica", "fsdp", None),
        P("fsdp", None),
        P("fsdp", None),
        P(),
    )
    return jax.shard_map(
        on_device,
        mesh=mesh,
        in_specs=placed,
        out_specs=(P("fsdp", None), P("fsdp", None)),
        check_vma=False,
    )
```

```python
import functools

import jax
import jax.numpy as jnp
from jax import lax
from jax.experimental import pallas as pl
from jax.experimental.pallas import tpu as pltpu
from jax.sharding import PartitionSpec as P

F32 = jnp.float32
BF16 = jnp.bfloat16
NN = (((1,), (0,)), ((), ()))
NT = (((1,), (1,)), ((), ()))


def mm(a, b, dims=NN):
    return lax.dot_general(a, b, dims, preferred_element_type=F32)


def split(x):
    top = x.astype(BF16)
    return top, (x - top.astype(F32)).astype(BF16)


def cost(flops, bytes_accessed):
    return pl.CostEstimate(flops=flops, bytes_accessed=bytes_accessed, transcendentals=0)


def front_kernel(factor, key_ref, grads_ref, a_ref, b_ref, top_ref, rest_ref):
    rank, width_k = a_ref.shape
    step = 256
    start = key_ref[0] + key_ref[1] * 1103515245
    r_index = lax.broadcasted_iota(jnp.int32, (rank, step), 0) * 374761393
    k_index = lax.broadcasted_iota(jnp.int32, (rank, step), 1) * 668265261
    base = r_index + k_index
    total = jnp.zeros((rank, grads_ref.shape[0]), F32)
    for k in range(0, width_k, step):
        shift = (k * 668265261 + 2**31) % 2**32 - 2**31
        hashed = base + (start + jnp.int32(shift))
        hashed = jnp.bitwise_xor(hashed, lax.shift_right_logical(hashed, jnp.int32(15)))
        hashed = hashed * 739982445
        hashed = jnp.bitwise_xor(hashed, lax.shift_right_logical(hashed, jnp.int32(12)))
        hashed = hashed * 695938361
        hashed = jnp.bitwise_xor(hashed, lax.shift_right_logical(hashed, jnp.int32(15)))
        high = jnp.bitwise_and(lax.shift_right_logical(hashed, jnp.int32(16)), 255).astype(F32)
        low = jnp.bitwise_and(lax.shift_right_logical(hashed, jnp.int32(8)), 255).astype(F32)
        part_a = ((high - 127.5) * 256.0).astype(BF16)
        part_b = (low - 127.5).astype(BF16)
        a_ref[:, k : k + step] = part_a
        b_ref[:, k : k + step] = part_b
        block = grads_ref[:, k : k + step]
        total += mm(part_a, block, NT) + mm(part_b, block, NT)
    top_ref[...], rest_ref[...] = split(factor * total)


def partial_kernel(factor, core_ref, own_ref, got_ref, gg_ref, a_ref, b_ref, top_ref, rest_ref, out_ref, tops, rests):
    tokens = own_ref.shape[0]

    @pl.when(pl.program_id(0) == 0)
    def _():
        other = factor * (mm(a_ref[...], gg_ref[...], NT) + mm(b_ref[...], gg_ref[...], NT))
        top, rest = split(other)
        tops[:, :tokens] = top_ref[...]
        tops[:, tokens:] = top
        rests[:, :tokens] = rest_ref[...]
        rests[:, tokens:] = rest

    acts = jnp.concatenate([own_ref[...], got_ref[...]], axis=0)
    out_ref[0] = (mm(tops[...], acts) + mm(rests[...], acts)).astype(BF16)


def side_kernel(unit, local_ref, anchor_ref, momentum_ref, a_ref, b_ref, local_term_ref, base_momentum_ref, base_anchor_ref):
    part_a, part_b = a_ref[...], b_ref[...]
    local = local_ref[...]
    local_term_ref[...] = unit * (mm(part_a, local, NT) + mm(part_b, local, NT))
    anchor = anchor_ref[...]
    top, rest = split(anchor)
    anchor_term = unit * (mm(top, part_a, NT) + mm(top, part_b, NT) + mm(rest, part_a, NT))
    base = 0.9 * momentum_ref[...] + anchor_term
    base_momentum_ref[...] = base
    top, rest = split(anchor_term + 0.9 * base)
    base_anchor_ref[...] = anchor - (0.7 * unit) * (mm(top, part_a) + mm(top, part_b) + mm(rest, part_a))


def last_kernel(unit, mean_ref, base_momentum_ref, base_anchor_ref, a_ref, b_ref, new_anchor_ref, new_momentum_ref):
    mean = mean_ref[...].astype(F32).T
    new_momentum_ref[...] = base_momentum_ref[...] + mean
    narrow = mean.astype(BF16)
    product = mm(narrow, a_ref[...]) + mm(narrow, b_ref[...])
    new_anchor_ref[...] = base_anchor_ref[...] - (0.7 * 1.9 * unit) * product


def limit(mib):
    return pltpu.CompilerParams(vmem_limit_bytes=mib << 20)


def total(x):
    return lax.reduce_precision(jnp.sum(x.astype(F32), axis=0), 8, 7).astype(BF16)


def groups(z_of, y_of):
    return [[z * 4 + y for z in zs for y in ys] for zs in z_of for ys in y_of]


def on_device(activations, grad_out, local_weight, anchor, momentum, projection_key):
    inputs, grads, local = activations[0], grad_out[0], local_weight[0]
    tokens, width = inputs.shape
    width_k, rank = grads.shape[1], momentum.shape[1]
    rows = anchor.shape[0]
    replicas, shards = lax.axis_size("replica"), lax.axis_size("fsdp")
    unit = (12.0 / float(rank)) ** 0.5 / 65536.0
    factor = unit * float(tokens * shards) ** (-0.5)
    chips = shards // 2
    core = lax.rem(lax.axis_index("fsdp"), 2).reshape(1)
    swap = [(i, i ^ 1) for i in range(shards)]
    same_core = [[2 * i + c for i in range(chips)] for c in range(2)]
    near = groups([range(h, h + 2) for h in range(0, 12, 2)], [range(4)])
    far = groups([range(l, 12, 2) for l in range(2)], [[y] for y in range(4)])
    shape = jax.ShapeDtypeStruct

    got = lax.ppermute(inputs, "fsdp", swap)
    got_grads = lax.ppermute(grads, "fsdp", swap)

    vmem = pl.BlockSpec(memory_space=pltpu.VMEM)
    part_a, part_b, top, rest = pl.pallas_call(
        functools.partial(front_kernel, factor),
        out_shape=(
            shape((rank, width_k), BF16),
            shape((rank, width_k), BF16),
            shape((rank, tokens), BF16),
            shape((rank, tokens), BF16),
        ),
        in_specs=[pl.BlockSpec(memory_space=pltpu.SMEM), vmem],
        out_specs=(vmem,) * 4,
        cost_estimate=cost(4 * rank * width_k * tokens, 4 * rank * width_k + 2 * tokens * width_k),
        compiler_params=limit(12),
        name="front",
    )(projection_key, grads)

    def whole(a, b):
        return pl.BlockSpec((a, b), lambda i, *_: (0, 0))

    pair = pl.BlockSpec((tokens, rows), lambda i, core: (0, 2 * i + core[0]))
    partial = pl.pallas_call(
        functools.partial(partial_kernel, factor),
        out_shape=shape((chips, rank, rows), BF16),
        grid_spec=pltpu.PrefetchScalarGridSpec(
            num_scalar_prefetch=1,
            grid=(chips,),
            in_specs=[
                pair,
                pair,
                whole(tokens, width_k),
                whole(rank, width_k),
                whole(rank, width_k),
                whole(rank, tokens),
                whole(rank, tokens),
            ],
            out_specs=pl.BlockSpec((1, rank, rows), lambda i, core: (i, 0, 0)),
            scratch_shapes=[pltpu.VMEM((rank, 2 * tokens), BF16)] * 2,
        ),
        cost_estimate=cost(8 * rank * tokens * width // 2, 2 * tokens * width + 2 * rank * rows * chips),
        compiler_params=limit(12),
        name="partial",
    )(core, inputs, got, got_grads, part_a, part_b, top, rest)

    landed = lax.all_to_all(partial, "fsdp", 0, 0, tiled=True, axis_index_groups=same_core)

    side_a, side_b, _ = lax.optimization_barrier((part_a, part_b, partial))
    tile = 128
    local_term, base_momentum, base_anchor = pl.pallas_call(
        functools.partial(side_kernel, unit),
        out_shape=(shape((rank, rows), F32), shape((rows, rank), F32), shape((rows, width_k), F32)),
        grid=(rows // tile,),
        in_specs=[
            pl.BlockSpec((tile, width_k), lambda i: (i, 0)),
            pl.BlockSpec((tile, width_k), lambda i: (i, 0)),
            pl.BlockSpec((tile, rank), lambda i: (i, 0)),
            whole(rank, width_k),
            whole(rank, width_k),
        ],
        out_specs=(
            pl.BlockSpec((rank, tile), lambda i: (0, i)),
            pl.BlockSpec((tile, rank), lambda i: (i, 0)),
            pl.BlockSpec((tile, width_k), lambda i: (i, 0)),
        ),
        cost_estimate=cost(16 * rank * rows * width_k, 10 * rows * width_k + 12 * rows * rank),
        compiler_params=limit(16),
        name="side",
    )(local, anchor, momentum, side_a, side_b)

    mine = (jnp.sum(landed.astype(F32), axis=0) - local_term) * (1.0 / replicas)
    pieces = lax.all_to_all(mine.astype(BF16).reshape(8, rank // 8, rows), "replica", 0, 0, tiled=True, axis_index_groups=near)
    piece = total(pieces)
    sixths = lax.all_to_all(jnp.broadcast_to(piece[None], (6,) + piece.shape), "replica", 0, 0, tiled=True, axis_index_groups=far)
    piece = total(sixths)
    mean = lax.all_to_all(jnp.broadcast_to(piece[None], (8,) + piece.shape), "replica", 0, 0, tiled=True, axis_index_groups=near)

    new_anchor, new_momentum = pl.pallas_call(
        functools.partial(last_kernel, unit),
        out_shape=(shape((rows, width_k), F32), shape((rows, rank), F32)),
        grid=(rows // tile,),
        in_specs=[
            pl.BlockSpec((rank, tile), lambda i: (0, i)),
            pl.BlockSpec((tile, rank), lambda i: (i, 0)),
            pl.BlockSpec((tile, width_k), lambda i: (i, 0)),
            whole(rank, width_k),
            whole(rank, width_k),
        ],
        out_specs=(
            pl.BlockSpec((tile, width_k), lambda i: (i, 0)),
            pl.BlockSpec((tile, rank), lambda i: (i, 0)),
        ),
        cost_estimate=cost(4 * rank * rows * width_k, 8 * rows * width_k + 10 * rows * rank),
        compiler_params=limit(16),
        name="last",
    )(mean.reshape(rank, rows), base_momentum, base_anchor, part_a, part_b)
    return (new_anchor, new_momentum)


def solution(mesh):
    placed = (
        P("replica", "fsdp", None),
        P("replica", "fsdp", None),
        P("replica", "fsdp", None),
        P("fsdp", None),
        P("fsdp", None),
        P(),
    )
    return jax.shard_map(
        on_device,
        mesh=mesh,
        in_specs=placed,
        out_specs=(P("fsdp", None), P("fsdp", None)),
        check_vma=False,
    )
```

```python
import functools

import jax
import jax.numpy as jnp
from jax import lax
from jax.experimental import pallas as pl
from jax.experimental.pallas import tpu as pltpu
from jax.sharding import PartitionSpec as P

F32 = jnp.float32
BF16 = jnp.bfloat16
NN = (((1,), (0,)), ((), ()))
NT = (((1,), (1,)), ((), ()))


def mm(a, b, dims=NN):
    return lax.dot_general(a, b, dims, preferred_element_type=F32)


def split(x):
    top = x.astype(BF16)
    return top, (x - top.astype(F32)).astype(BF16)


def cost(flops, bytes_accessed):
    return pl.CostEstimate(flops=flops, bytes_accessed=bytes_accessed, transcendentals=0)


def front_kernel(factor, key_hbm, grads_hbm, a_ref, b_ref, top_ref, rest_ref, key_ref, grads_ref, sems):
    key_copy = pltpu.make_async_copy(key_hbm, key_ref, sems.at[0])
    grads_copy = pltpu.make_async_copy(grads_hbm, grads_ref, sems.at[1])
    key_copy.start()
    grads_copy.start()
    rank, width_k = a_ref.shape
    step = 256
    r_index = lax.broadcasted_iota(jnp.int32, (rank, step), 0) * 374761393
    k_index = lax.broadcasted_iota(jnp.int32, (rank, step), 1) * 668265261
    base = r_index + k_index
    key_copy.wait()
    start = key_ref[0] + key_ref[1] * 1103515245
    for k in range(0, width_k, step):
        shift = (k * 668265261 + 2**31) % 2**32 - 2**31
        hashed = base + (start + jnp.int32(shift))
        hashed = jnp.bitwise_xor(hashed, lax.shift_right_logical(hashed, jnp.int32(15)))
        hashed = hashed * 739982445
        hashed = jnp.bitwise_xor(hashed, lax.shift_right_logical(hashed, jnp.int32(12)))
        hashed = hashed * 695938361
        hashed = jnp.bitwise_xor(hashed, lax.shift_right_logical(hashed, jnp.int32(15)))
        high = jnp.bitwise_and(lax.shift_right_logical(hashed, jnp.int32(16)), 255).astype(F32)
        low = jnp.bitwise_and(lax.shift_right_logical(hashed, jnp.int32(8)), 255).astype(F32)
        a_ref[:, k : k + step] = ((high - 127.5) * 256.0).astype(BF16)
        b_ref[:, k : k + step] = (low - 127.5).astype(BF16)
    grads_copy.wait()
    grads = grads_ref[...]
    top_ref[...], rest_ref[...] = split(factor * (mm(a_ref[...], grads, NT) + mm(b_ref[...], grads, NT)))


def partial_kernel(factor, own_hbm, got_hbm, gg_hbm, a_ref, b_ref, top_ref, rest_ref, out_hbm, acts, grads, tops, rests, sums, own_sems, got_sems, out_sems, gg_sem):
    chips, both, rows = acts.shape
    tokens = both // 2
    core = lax.rem(lax.axis_index("fsdp"), 2)
    gg_copy = pltpu.make_async_copy(gg_hbm, grads, gg_sem)
    gg_copy.start()
    loads = []
    for i in range(chips):
        columns = pl.ds(pl.multiple_of((2 * i + core) * rows, rows), rows)
        own = pltpu.make_async_copy(own_hbm.at[:, columns], acts.at[i, pl.ds(0, tokens)], own_sems.at[i])
        got = pltpu.make_async_copy(got_hbm.at[:, columns], acts.at[i, pl.ds(tokens, tokens)], got_sems.at[i])
        own.start()
        got.start()
        loads.append((own, got))
    gg_copy.wait()
    block = grads[...]
    top, rest = split(factor * (mm(a_ref[...], block, NT) + mm(b_ref[...], block, NT)))
    tops[:, :tokens] = top_ref[...]
    tops[:, tokens:] = top
    rests[:, :tokens] = rest_ref[...]
    rests[:, tokens:] = rest
    stores = []
    for i in range(chips):
        for load in loads[i]:
            load.wait()
        sums[i] = (mm(tops[...], acts[i]) + mm(rests[...], acts[i])).astype(BF16)
        store = pltpu.make_async_copy(sums.at[i], out_hbm.at[i], out_sems.at[i])
        store.start()
        stores.append(store)
    for store in stores:
        store.wait()


def sum_kernel(portion, landed_hbm, local_hbm, out_ref, landed, local_ref, local_sem, sems):
    chips, rank, rows = landed.shape
    local_copy = pltpu.make_async_copy(local_hbm, local_ref, local_sem)
    local_copy.start()
    loads = []
    parts = 4
    piece = rank // parts
    for p in range(parts):
        span = pl.ds(p * piece, piece)
        load = pltpu.make_async_copy(landed_hbm.at[:, span], landed.at[:, span], sems.at[p])
        load.start()
        loads.append(load)
    local_copy.wait()
    for p in range(parts):
        span = pl.ds(p * piece, piece)
        loads[p].wait()
        added = landed[0, span].astype(F32)
        for i in range(1, chips):
            added += landed[i, span].astype(F32)
        out_ref[span] = ((added - local_ref[span]) * portion).astype(BF16)


def side_kernel(unit, local_ref, anchor_ref, momentum_ref, a_ref, b_ref, local_term_ref, base_momentum_ref, base_anchor_ref):
    part_a, part_b = a_ref[...], b_ref[...]
    local = local_ref[...]
    local_term_ref[...] = unit * (mm(part_a, local, NT) + mm(part_b, local, NT))
    anchor = anchor_ref[...]
    top, rest = split(anchor)
    anchor_term = unit * (mm(top, part_a, NT) + mm(top, part_b, NT) + mm(rest, part_a, NT))
    base = 0.9 * momentum_ref[...] + anchor_term
    base_momentum_ref[...] = base
    top, rest = split(anchor_term + 0.9 * base)
    base_anchor_ref[...] = anchor - (0.7 * unit) * (mm(top, part_a) + mm(top, part_b) + mm(rest, part_a))


def last_kernel(unit, mean_ref, base_momentum_ref, base_anchor_ref, a_ref, b_ref, new_anchor_hbm, new_momentum_ref, outs, sems):
    tile = outs.shape[1]
    stores = []
    for i in range(outs.shape[0]):
        span = pl.ds(i * tile, tile)
        mean = mean_ref[:, span].astype(F32).T
        new_momentum_ref[span] = base_momentum_ref[span] + mean
        narrow = mean.astype(BF16)
        product = mm(narrow, a_ref[...]) + mm(narrow, b_ref[...])
        outs[i] = base_anchor_ref[span] - (0.7 * 1.9 * unit) * product
        store = pltpu.make_async_copy(outs.at[i], new_anchor_hbm.at[span], sems.at[i])
        store.start()
        stores.append(store)
    for store in stores:
        store.wait()


def limit(mib):
    return pltpu.CompilerParams(vmem_limit_bytes=mib << 20)


def total(x):
    return lax.reduce_precision(jnp.sum(x.astype(F32), axis=0), 8, 7).astype(BF16)


def groups(z_of, y_of):
    return [[z * 4 + y for z in zs for y in ys] for zs in z_of for ys in y_of]


def on_device(activations, grad_out, local_weight, anchor, momentum, projection_key):
    inputs, grads, local = activations[0], grad_out[0], local_weight[0]
    tokens, width = inputs.shape
    width_k, rank = grads.shape[1], momentum.shape[1]
    rows = anchor.shape[0]
    replicas, shards = lax.axis_size("replica"), lax.axis_size("fsdp")
    unit = (12.0 / float(rank)) ** 0.5 / 65536.0
    factor = unit * float(tokens * shards) ** (-0.5)
    chips = shards // 2
    swap = [(i, i ^ 1) for i in range(shards)]
    same_core = [[2 * i + c for i in range(chips)] for c in range(2)]
    near = groups([range(h, h + 2) for h in range(0, 12, 2)], [range(4)])
    far = groups([range(l, 12, 2) for l in range(2)], [[y] for y in range(4)])
    shape = jax.ShapeDtypeStruct

    held = pltpu.with_memory_space_constraint(inputs, pltpu.HBM)
    held_grads = pltpu.with_memory_space_constraint(grads, pltpu.HBM)
    held_key = pltpu.with_memory_space_constraint(projection_key, pltpu.HBM)
    got = lax.ppermute(inputs, "fsdp", swap)
    got_grads = lax.ppermute(grads, "fsdp", swap)

    vmem = pl.BlockSpec(memory_space=pltpu.VMEM)
    hbm = pl.BlockSpec(memory_space=pltpu.HBM)
    free = pl.BlockSpec(memory_space=pl.ANY)
    dma = pltpu.SemaphoreType.DMA
    part_a, part_b, top, rest = pl.pallas_call(
        functools.partial(front_kernel, factor),
        out_shape=(
            shape((rank, width_k), BF16),
            shape((rank, width_k), BF16),
            shape((rank, tokens), BF16),
            shape((rank, tokens), BF16),
        ),
        in_specs=[hbm, hbm],
        out_specs=(vmem,) * 4,
        scratch_shapes=[pltpu.SMEM((2,), jnp.int32), pltpu.VMEM((tokens, width_k), BF16), dma((2,))],
        cost_estimate=cost(4 * rank * width_k * tokens, 4 * rank * width_k + 2 * tokens * width_k),
        compiler_params=limit(12),
        name="front",
    )(held_key, held_grads)

    def whole(a, b):
        return pl.BlockSpec((a, b), lambda i, *_: (0, 0))

    partial = pl.pallas_call(
        functools.partial(partial_kernel, factor),
        out_shape=pltpu.HBM((chips, rank, rows), BF16),
        in_specs=[hbm, free, free, vmem, vmem, vmem, vmem],
        out_specs=free,
        scratch_shapes=[
            pltpu.VMEM((chips, 2 * tokens, rows), BF16),
            pltpu.VMEM((tokens, width_k), BF16),
            pltpu.VMEM((rank, 2 * tokens), BF16),
            pltpu.VMEM((rank, 2 * tokens), BF16),
            pltpu.VMEM((chips, rank, rows), BF16),
            dma((chips,)),
            dma((chips,)),
            dma((chips,)),
            dma,
        ],
        cost_estimate=cost(8 * rank * tokens * width // 2, 2 * tokens * width + 2 * rank * rows * chips),
        compiler_params=limit(16),
        name="partial",
    )(held, got, got_grads, part_a, part_b, top, rest)

    landed = lax.all_to_all(partial, "fsdp", 0, 0, tiled=True, axis_index_groups=same_core)

    side_a, side_b, _ = lax.optimization_barrier((part_a, part_b, partial))
    tile = 128
    local_term, base_momentum, base_anchor = pl.pallas_call(
        functools.partial(side_kernel, unit),
        out_shape=(pltpu.HBM((rank, rows), F32), shape((rows, rank), F32), shape((rows, width_k), F32)),
        grid=(rows // tile,),
        in_specs=[
            pl.BlockSpec((tile, width_k), lambda i: (i, 0)),
            pl.BlockSpec((tile, width_k), lambda i: (i, 0)),
            pl.BlockSpec((tile, rank), lambda i: (i, 0)),
            whole(rank, width_k),
            whole(rank, width_k),
        ],
        out_specs=(
            pl.BlockSpec((rank, tile), lambda i: (0, i)),
            pl.BlockSpec((tile, rank), lambda i: (i, 0)),
            pl.BlockSpec((tile, width_k), lambda i: (i, 0)),
        ),
        cost_estimate=cost(16 * rank * rows * width_k, 10 * rows * width_k + 12 * rows * rank),
        compiler_params=limit(16),
        name="side",
    )(local, anchor, momentum, side_a, side_b)

    mine = pl.pallas_call(
        functools.partial(sum_kernel, 1.0 / replicas),
        out_shape=shape((rank, rows), BF16),
        in_specs=[free, hbm],
        out_specs=vmem,
        scratch_shapes=[pltpu.VMEM((chips, rank, rows), BF16), pltpu.VMEM((rank, rows), F32), dma, dma((4,))],
        cost_estimate=cost(chips * rank * rows, 2 * (chips + 3) * rank * rows),
        compiler_params=limit(12),
        name="gather_sum",
    )(landed, pltpu.with_memory_space_constraint(local_term, pltpu.HBM))
    pieces = lax.all_to_all(mine.reshape(8, rank // 8, rows), "replica", 0, 0, tiled=True, axis_index_groups=near)
    piece = total(pieces)
    sixths = lax.all_to_all(jnp.broadcast_to(piece[None], (6,) + piece.shape), "replica", 0, 0, tiled=True, axis_index_groups=far)
    piece = total(sixths)
    mean = lax.all_to_all(jnp.broadcast_to(piece[None], (8,) + piece.shape), "replica", 0, 0, tiled=True, axis_index_groups=near)

    new_anchor, new_momentum = pl.pallas_call(
        functools.partial(last_kernel, unit),
        out_shape=(pltpu.HBM((rows, width_k), F32), shape((rows, rank), F32)),
        in_specs=[vmem] * 5,
        out_specs=(hbm, vmem),
        scratch_shapes=[pltpu.VMEM((rows // tile, tile, width_k), F32), dma((rows // tile,))],
        cost_estimate=cost(4 * rank * rows * width_k, 8 * rows * width_k + 10 * rows * rank),
        compiler_params=limit(16),
        name="last",
    )(mean.reshape(rank, rows), base_momentum, base_anchor, part_a, part_b)
    return (new_anchor, new_momentum)


def solution(mesh):
    placed = (
        P("replica", "fsdp", None),
        P("replica", "fsdp", None),
        P("replica", "fsdp", None),
        P("fsdp", None),
        P("fsdp", None),
        P(),
    )
    return jax.shard_map(
        on_device,
        mesh=mesh,
        in_specs=placed,
        out_specs=(P("fsdp", None), P("fsdp", None)),
        check_vma=False,
    )
```

```python
import functools

import jax
import jax.numpy as jnp
from jax import lax
from jax.experimental import pallas as pl
from jax.experimental.pallas import tpu as pltpu
from jax.sharding import PartitionSpec as P

F32 = jnp.float32
BF16 = jnp.bfloat16
NN = (((1,), (0,)), ((), ()))
NT = (((1,), (1,)), ((), ()))


def mm(a, b, dims=NN):
    return lax.dot_general(a, b, dims, preferred_element_type=F32)


def split(x):
    top = x.astype(BF16)
    return top, (x - top.astype(F32)).astype(BF16)


def cost(flops, bytes_accessed):
    return pl.CostEstimate(flops=flops, bytes_accessed=bytes_accessed, transcendentals=0)


def front_kernel(factor, key_hbm, grads_hbm, a_ref, b_ref, top_ref, rest_ref, key_ref, grads_ref, sems):
    key_copy = pltpu.make_async_copy(key_hbm, key_ref, sems.at[0])
    grads_copy = pltpu.make_async_copy(grads_hbm, grads_ref, sems.at[1])
    key_copy.start()
    grads_copy.start()
    rank, width_k = a_ref.shape
    step = 256
    r_index = lax.broadcasted_iota(jnp.int32, (rank, step), 0) * 374761393
    k_index = lax.broadcasted_iota(jnp.int32, (rank, step), 1) * 668265261
    base = r_index + k_index
    key_copy.wait()
    start = key_ref[0] + key_ref[1] * 1103515245
    for k in range(0, width_k, step):
        shift = (k * 668265261 + 2**31) % 2**32 - 2**31
        hashed = base + (start + jnp.int32(shift))
        hashed = jnp.bitwise_xor(hashed, lax.shift_right_logical(hashed, jnp.int32(15)))
        hashed = hashed * 739982445
        hashed = jnp.bitwise_xor(hashed, lax.shift_right_logical(hashed, jnp.int32(12)))
        hashed = hashed * 695938361
        hashed = jnp.bitwise_xor(hashed, lax.shift_right_logical(hashed, jnp.int32(15)))
        high = jnp.bitwise_and(lax.shift_right_logical(hashed, jnp.int32(16)), 255).astype(F32)
        low = jnp.bitwise_and(lax.shift_right_logical(hashed, jnp.int32(8)), 255).astype(F32)
        a_ref[:, k : k + step] = ((high - 127.5) * 256.0).astype(BF16)
        b_ref[:, k : k + step] = (low - 127.5).astype(BF16)
    grads_copy.wait()
    grads = grads_ref[...]
    top_ref[...], rest_ref[...] = split(factor * (mm(a_ref[...], grads, NT) + mm(b_ref[...], grads, NT)))


def partial_kernel(factor, own_hbm, got_hbm, gg_hbm, a_ref, b_ref, top_ref, rest_ref, out_hbm, acts, grads, tops, sums, own_sems, got_sems, out_sems, gg_sem):
    chips, tokens, rows = acts.shape
    tokens = tokens // 2
    core = lax.rem(lax.axis_index("fsdp"), 2)
    gg_copy = pltpu.make_async_copy(gg_hbm, grads, gg_sem)
    gg_copy.start()
    loads = []
    for i in range(chips):
        columns = pl.ds(pl.multiple_of((2 * i + core) * rows, rows), rows)
        own = pltpu.make_async_copy(own_hbm.at[:, columns], acts.at[i, pl.ds(0, tokens)], own_sems.at[i])
        got = pltpu.make_async_copy(got_hbm.at[:, columns], acts.at[i, pl.ds(tokens, tokens)], got_sems.at[i])
        own.start()
        got.start()
        loads.append((own, got))
    gg_copy.wait()
    rank = a_ref.shape[0]
    both = mm(jnp.concatenate([a_ref[...], b_ref[...]], axis=0), grads[...], NT)
    top, rest = split(factor * (both[:rank] + both[rank:]))
    tops[:rank, :tokens] = top_ref[...]
    tops[:rank, tokens:] = top
    tops[rank:, :tokens] = rest_ref[...]
    tops[rank:, tokens:] = rest
    stores = []
    for i in range(chips):
        for load in loads[i]:
            load.wait()
        product = mm(tops[...], acts[i])
        sums[i] = (product[:rank] + product[rank:]).astype(BF16)
        store = pltpu.make_async_copy(sums.at[i], out_hbm.at[i], out_sems.at[i])
        store.start()
        stores.append(store)
    for store in stores:
        store.wait()


def sum_kernel(portion, landed_hbm, local_hbm, out_ref, landed, local_ref, local_sem, sems):
    chips, rank, rows = landed.shape
    local_copy = pltpu.make_async_copy(local_hbm, local_ref, local_sem)
    local_copy.start()
    loads = []
    parts = 4
    piece = rank // parts
    for p in range(parts):
        span = pl.ds(p * piece, piece)
        load = pltpu.make_async_copy(landed_hbm.at[:, span], landed.at[:, span], sems.at[p])
        load.start()
        loads.append(load)
    local_copy.wait()
    for p in range(parts):
        span = pl.ds(p * piece, piece)
        loads[p].wait()
        added = landed[0, span].astype(F32)
        for i in range(1, chips):
            added += landed[i, span].astype(F32)
        out_ref[span] = ((added - local_ref[span]) * portion).astype(BF16)


def side_kernel(unit, local_ref, anchor_ref, momentum_ref, a_ref, b_ref, local_term_ref, base_momentum_ref, base_anchor_ref):
    part_a, part_b = a_ref[...], b_ref[...]
    local = local_ref[...]
    local_term_ref[...] = unit * (mm(part_a, local, NT) + mm(part_b, local, NT))
    anchor = anchor_ref[...]
    top, rest = split(anchor)
    anchor_term = unit * (mm(top, part_a, NT) + mm(top, part_b, NT) + mm(rest, part_a, NT))
    base = 0.9 * momentum_ref[...] + anchor_term
    base_momentum_ref[...] = base
    top, rest = split(anchor_term + 0.9 * base)
    base_anchor_ref[...] = anchor - (0.7 * unit) * (mm(top, part_a) + mm(top, part_b) + mm(rest, part_a))


def last_kernel(unit, mean_ref, base_momentum_ref, base_anchor_ref, a_ref, b_ref, new_anchor_hbm, new_momentum_ref, outs, sems):
    tile = outs.shape[1]
    stores = []
    for i in range(outs.shape[0]):
        span = pl.ds(i * tile, tile)
        mean = mean_ref[:, span].astype(F32).T
        new_momentum_ref[span] = base_momentum_ref[span] + mean
        narrow = mean.astype(BF16)
        product = mm(narrow, a_ref[...]) + mm(narrow, b_ref[...])
        outs[i] = base_anchor_ref[span] - (0.7 * 1.9 * unit) * product
        store = pltpu.make_async_copy(outs.at[i], new_anchor_hbm.at[span], sems.at[i])
        store.start()
        stores.append(store)
    for store in stores:
        store.wait()


def limit(mib):
    return pltpu.CompilerParams(vmem_limit_bytes=mib << 20)


def total(x):
    return lax.reduce_precision(jnp.sum(x.astype(F32), axis=0), 8, 7).astype(BF16)


def groups(z_of, y_of):
    return [[z * 4 + y for z in zs for y in ys] for zs in z_of for ys in y_of]


def on_device(activations, grad_out, local_weight, anchor, momentum, projection_key):
    inputs, grads, local = activations[0], grad_out[0], local_weight[0]
    tokens, width = inputs.shape
    width_k, rank = grads.shape[1], momentum.shape[1]
    rows = anchor.shape[0]
    replicas, shards = lax.axis_size("replica"), lax.axis_size("fsdp")
    unit = (12.0 / float(rank)) ** 0.5 / 65536.0
    factor = unit * float(tokens * shards) ** (-0.5)
    chips = shards // 2
    swap = [(i, i ^ 1) for i in range(shards)]
    same_core = [[2 * i + c for i in range(chips)] for c in range(2)]
    near = groups([range(h, h + 4) for h in range(0, 12, 4)], [[0, 1], [3, 2]])
    far = groups([range(l, 12, 4) for l in range(4)], [[0, 3], [1, 2]])
    shape = jax.ShapeDtypeStruct

    held = pltpu.with_memory_space_constraint(inputs, pltpu.HBM)
    held_grads = pltpu.with_memory_space_constraint(grads, pltpu.HBM)
    held_key = pltpu.with_memory_space_constraint(projection_key, pltpu.HBM)
    got = lax.ppermute(inputs, "fsdp", swap)
    got_grads = lax.ppermute(grads, "fsdp", swap)

    vmem = pl.BlockSpec(memory_space=pltpu.VMEM)
    hbm = pl.BlockSpec(memory_space=pltpu.HBM)
    free = pl.BlockSpec(memory_space=pl.ANY)
    dma = pltpu.SemaphoreType.DMA
    part_a, part_b, top, rest = pl.pallas_call(
        functools.partial(front_kernel, factor),
        out_shape=(
            shape((rank, width_k), BF16),
            shape((rank, width_k), BF16),
            shape((rank, tokens), BF16),
            shape((rank, tokens), BF16),
        ),
        in_specs=[hbm, hbm],
        out_specs=(vmem,) * 4,
        scratch_shapes=[pltpu.SMEM((2,), jnp.int32), pltpu.VMEM((tokens, width_k), BF16), dma((2,))],
        cost_estimate=cost(4 * rank * width_k * tokens, 4 * rank * width_k + 2 * tokens * width_k),
        compiler_params=limit(12),
        name="front",
    )(held_key, held_grads)

    def whole(a, b):
        return pl.BlockSpec((a, b), lambda i, *_: (0, 0))

    partial = pl.pallas_call(
        functools.partial(partial_kernel, factor),
        out_shape=pltpu.HBM((chips, rank, rows), BF16),
        in_specs=[hbm, free, free, vmem, vmem, vmem, vmem],
        out_specs=free,
        scratch_shapes=[
            pltpu.VMEM((chips, 2 * tokens, rows), BF16),
            pltpu.VMEM((tokens, width_k), BF16),
            pltpu.VMEM((2 * rank, 2 * tokens), BF16),
            pltpu.VMEM((chips, rank, rows), BF16),
            dma((chips,)),
            dma((chips,)),
            dma((chips,)),
            dma,
        ],
        cost_estimate=cost(8 * rank * tokens * width // 2, 2 * tokens * width + 2 * rank * rows * chips),
        compiler_params=limit(16),
        name="partial",
    )(held, got, got_grads, part_a, part_b, top, rest)

    landed = lax.all_to_all(partial, "fsdp", 0, 0, tiled=True, axis_index_groups=same_core)

    side_a, side_b, _ = lax.optimization_barrier((part_a, part_b, partial))
    tile = 128
    local_term, base_momentum, base_anchor = pl.pallas_call(
        functools.partial(side_kernel, unit),
        out_shape=(pltpu.HBM((rank, rows), F32), shape((rows, rank), F32), shape((rows, width_k), F32)),
        grid=(rows // tile,),
        in_specs=[
            pl.BlockSpec((tile, width_k), lambda i: (i, 0)),
            pl.BlockSpec((tile, width_k), lambda i: (i, 0)),
            pl.BlockSpec((tile, rank), lambda i: (i, 0)),
            whole(rank, width_k),
            whole(rank, width_k),
        ],
        out_specs=(
            pl.BlockSpec((rank, tile), lambda i: (0, i)),
            pl.BlockSpec((tile, rank), lambda i: (i, 0)),
            pl.BlockSpec((tile, width_k), lambda i: (i, 0)),
        ),
        cost_estimate=cost(16 * rank * rows * width_k, 10 * rows * width_k + 12 * rows * rank),
        compiler_params=limit(16),
        name="side",
    )(local, anchor, momentum, side_a, side_b)

    mine = pl.pallas_call(
        functools.partial(sum_kernel, 1.0 / replicas),
        out_shape=shape((rank, rows), BF16),
        in_specs=[free, hbm],
        out_specs=vmem,
        scratch_shapes=[pltpu.VMEM((chips, rank, rows), BF16), pltpu.VMEM((rank, rows), F32), dma, dma((4,))],
        cost_estimate=cost(chips * rank * rows, 2 * (chips + 3) * rank * rows),
        compiler_params=limit(12),
        name="gather_sum",
    )(landed, pltpu.with_memory_space_constraint(local_term, pltpu.HBM))
    pieces = lax.all_to_all(mine.reshape(8, rank // 8, rows), "replica", 0, 0, tiled=True, axis_index_groups=near)
    piece = total(pieces)
    sixths = lax.all_to_all(jnp.broadcast_to(piece[None], (6,) + piece.shape), "replica", 0, 0, tiled=True, axis_index_groups=far)
    piece = total(sixths)
    mean = lax.all_to_all(jnp.broadcast_to(piece[None], (8,) + piece.shape), "replica", 0, 0, tiled=True, axis_index_groups=near)

    new_anchor, new_momentum = pl.pallas_call(
        functools.partial(last_kernel, unit),
        out_shape=(pltpu.HBM((rows, width_k), F32), shape((rows, rank), F32)),
        in_specs=[vmem] * 5,
        out_specs=(hbm, vmem),
        scratch_shapes=[pltpu.VMEM((rows // tile, tile, width_k), F32), dma((rows // tile,))],
        cost_estimate=cost(4 * rank * rows * width_k, 8 * rows * width_k + 10 * rows * rank),
        compiler_params=limit(16),
        name="last",
    )(mean.reshape(rank, rows), base_momentum, base_anchor, part_a, part_b)
    return (new_anchor, new_momentum)


def solution(mesh):
    placed = (
        P("replica", "fsdp", None),
        P("replica", "fsdp", None),
        P("replica", "fsdp", None),
        P("fsdp", None),
        P("fsdp", None),
        P(),
    )
    return jax.shard_map(
        on_device,
        mesh=mesh,
        in_specs=placed,
        out_specs=(P("fsdp", None), P("fsdp", None)),
        check_vma=False,
    )
```

```python
import functools

import jax
import jax.numpy as jnp
from jax import lax
from jax.experimental import pallas as pl
from jax.experimental.pallas import tpu as pltpu
from jax.sharding import PartitionSpec as P

F32 = jnp.float32
BF16 = jnp.bfloat16
NN = (((1,), (0,)), ((), ()))
NT = (((1,), (1,)), ((), ()))


def mm(a, b, dims=NN):
    return lax.dot_general(a, b, dims, preferred_element_type=F32)


def split(x):
    top = x.astype(BF16)
    return top, (x - top.astype(F32)).astype(BF16)


def cost(flops, bytes_accessed):
    return pl.CostEstimate(flops=flops, bytes_accessed=bytes_accessed, transcendentals=0)


def front_kernel(factor, key_hbm, grads_hbm, acts_hbm, a_ref, b_ref, top_ref, rest_ref, pack_hbm, key_ref, grads_ref, pack, sems, give_sems):
    key_copy = pltpu.make_async_copy(key_hbm, key_ref, sems.at[0])
    grads_copy = pltpu.make_async_copy(grads_hbm, grads_ref, sems.at[1])
    key_copy.start()
    grads_copy.start()
    rank, width_k = a_ref.shape
    tokens, given = grads_ref.shape[0], pack.shape[1] - 2 * rank
    chips = give_sems.shape[0]
    rows = given // chips
    other = 1 - lax.rem(lax.axis_index("fsdp"), 2)
    gives = []
    for i in range(chips):
        columns = pl.ds(pl.multiple_of((2 * i + other) * rows, rows), rows)
        give = pltpu.make_async_copy(acts_hbm.at[:, columns], pack.at[:, pl.ds(i * rows, rows)], give_sems.at[i])
        give.start()
        gives.append(give)
    acts_out = pltpu.make_async_copy(pack.at[:, pl.ds(0, given)], pack_hbm.at[:, pl.ds(0, given)], sems.at[2])
    last_out = pltpu.make_async_copy(pack.at[:, pl.ds(given, 2 * rank)], pack_hbm.at[:, pl.ds(given, 2 * rank)], sems.at[3])
    step = 256
    r_index = lax.broadcasted_iota(jnp.int32, (rank, step), 0) * 374761393
    k_index = lax.broadcasted_iota(jnp.int32, (rank, step), 1) * 668265261
    base = r_index + k_index
    key_copy.wait()
    start = key_ref[0] + key_ref[1] * 1103515245
    for k in range(0, width_k, step):
        shift = (k * 668265261 + 2**31) % 2**32 - 2**31
        hashed = base + (start + jnp.int32(shift))
        hashed = jnp.bitwise_xor(hashed, lax.shift_right_logical(hashed, jnp.int32(15)))
        hashed = hashed * 739982445
        hashed = jnp.bitwise_xor(hashed, lax.shift_right_logical(hashed, jnp.int32(12)))
        hashed = hashed * 695938361
        hashed = jnp.bitwise_xor(hashed, lax.shift_right_logical(hashed, jnp.int32(15)))
        high = jnp.bitwise_and(lax.shift_right_logical(hashed, jnp.int32(16)), 255).astype(F32)
        low = jnp.bitwise_and(lax.shift_right_logical(hashed, jnp.int32(8)), 255).astype(F32)
        a_ref[:, k : k + step] = ((high - 127.5) * 256.0).astype(BF16)
        b_ref[:, k : k + step] = (low - 127.5).astype(BF16)
        if k == step:
            for give in gives:
                give.wait()
            acts_out.start()
    grads_copy.wait()
    grads = grads_ref[...]
    top, rest = split(factor * (mm(a_ref[...], grads, NT) + mm(b_ref[...], grads, NT)))
    top_ref[...] = top
    rest_ref[...] = rest
    for j in range(rank // tokens):
        piece = slice(j * tokens, (j + 1) * tokens)
        pack[:, given + j * tokens : given + (j + 1) * tokens] = top[piece]
        pack[:, given + rank + j * tokens : given + rank + (j + 1) * tokens] = rest[piece]
    last_out.start()
    acts_out.wait()
    last_out.wait()


def partial_kernel(own_hbm, got_hbm, top_ref, rest_ref, out_hbm, acts, theirs, tops, sums, own_sems, got_sems, out_sems, last_sem):
    chips, both, rows = acts.shape
    rank, tokens = top_ref.shape
    core = lax.rem(lax.axis_index("fsdp"), 2)
    given = chips * rows
    last = pltpu.make_async_copy(got_hbm.at[:, pl.ds(given, 2 * rank)], theirs, last_sem)
    last.start()
    loads = []
    for i in range(chips):
        columns = pl.ds(pl.multiple_of((2 * i + core) * rows, rows), rows)
        own = pltpu.make_async_copy(own_hbm.at[:, columns], acts.at[i, pl.ds(0, tokens)], own_sems.at[i])
        got = pltpu.make_async_copy(got_hbm.at[:, pl.ds(i * rows, rows)], acts.at[i, pl.ds(tokens, tokens)], got_sems.at[i])
        own.start()
        got.start()
        loads.append((own, got))
    tops[:rank, :tokens] = top_ref[...]
    tops[rank:, :tokens] = rest_ref[...]
    last.wait()
    for j in range(2 * rank // tokens):
        tops[j * tokens : (j + 1) * tokens, tokens:] = theirs[:, j * tokens : (j + 1) * tokens]
    stores = []
    for i in range(chips):
        for load in loads[i]:
            load.wait()
        product = mm(tops[...], acts[i])
        sums[i] = (product[:rank] + product[rank:]).astype(BF16)
        store = pltpu.make_async_copy(sums.at[i], out_hbm.at[i], out_sems.at[i])
        store.start()
        stores.append(store)
    for store in stores:
        store.wait()


def sum_kernel(portion, landed_hbm, local_hbm, out_ref, landed, local_ref, local_sem, sems):
    chips, rank, rows = landed.shape
    local_copy = pltpu.make_async_copy(local_hbm, local_ref, local_sem)
    local_copy.start()
    loads = []
    parts = 4
    piece = rank // parts
    for p in range(parts):
        span = pl.ds(p * piece, piece)
        load = pltpu.make_async_copy(landed_hbm.at[:, span], landed.at[:, span], sems.at[p])
        load.start()
        loads.append(load)
    local_copy.wait()
    for p in range(parts):
        span = pl.ds(p * piece, piece)
        loads[p].wait()
        added = landed[0, span].astype(F32)
        for i in range(1, chips):
            added += landed[i, span].astype(F32)
        out_ref[span] = ((added - local_ref[span]) * portion).astype(BF16)


def side_kernel(unit, local_ref, anchor_ref, momentum_ref, a_ref, b_ref, local_term_ref, base_momentum_ref, base_anchor_ref):
    part_a, part_b = a_ref[...], b_ref[...]
    local = local_ref[...]
    local_term_ref[...] = unit * (mm(part_a, local, NT) + mm(part_b, local, NT))
    anchor = anchor_ref[...]
    top, rest = split(anchor)
    anchor_term = unit * (mm(top, part_a, NT) + mm(top, part_b, NT) + mm(rest, part_a, NT))
    base = 0.9 * momentum_ref[...] + anchor_term
    base_momentum_ref[...] = base
    top, rest = split(anchor_term + 0.9 * base)
    base_anchor_ref[...] = anchor - (0.7 * unit) * (mm(top, part_a) + mm(top, part_b) + mm(rest, part_a))


def last_kernel(unit, mean_ref, base_momentum_ref, base_anchor_ref, a_ref, b_ref, new_anchor_hbm, new_momentum_ref, outs, sems):
    tile = outs.shape[1]
    stores = []
    for i in range(outs.shape[0]):
        span = pl.ds(i * tile, tile)
        mean = mean_ref[:, span].astype(F32).T
        new_momentum_ref[span] = base_momentum_ref[span] + mean
        narrow = mean.astype(BF16)
        product = mm(narrow, a_ref[...]) + mm(narrow, b_ref[...])
        outs[i] = base_anchor_ref[span] - (0.7 * 1.9 * unit) * product
        store = pltpu.make_async_copy(outs.at[i], new_anchor_hbm.at[span], sems.at[i])
        store.start()
        stores.append(store)
    for store in stores:
        store.wait()


def limit(mib):
    return pltpu.CompilerParams(vmem_limit_bytes=mib << 20)


def total(x):
    return lax.reduce_precision(jnp.sum(x.astype(F32), axis=0), 8, 7).astype(BF16)


def groups(z_of, y_of):
    return [[z * 4 + y for z in zs for y in ys] for zs in z_of for ys in y_of]


def on_device(activations, grad_out, local_weight, anchor, momentum, projection_key):
    inputs, grads, local = activations[0], grad_out[0], local_weight[0]
    tokens, width = inputs.shape
    width_k, rank = grads.shape[1], momentum.shape[1]
    rows = anchor.shape[0]
    replicas, shards = lax.axis_size("replica"), lax.axis_size("fsdp")
    unit = (12.0 / float(rank)) ** 0.5 / 65536.0
    factor = unit * float(tokens * shards) ** (-0.5)
    chips = shards // 2
    swap = [(i, i ^ 1) for i in range(shards)]
    same_core = [[2 * i + c for i in range(chips)] for c in range(2)]
    near = groups([range(h, h + 4) for h in range(0, 12, 4)], [[0, 1], [3, 2]])
    far = groups([range(l, 12, 4) for l in range(4)], [[0, 3], [1, 2]])
    shape = jax.ShapeDtypeStruct

    held = pltpu.with_memory_space_constraint(inputs, pltpu.HBM)
    held_grads = pltpu.with_memory_space_constraint(grads, pltpu.HBM)
    held_key = pltpu.with_memory_space_constraint(projection_key, pltpu.HBM)

    vmem = pl.BlockSpec(memory_space=pltpu.VMEM)
    hbm = pl.BlockSpec(memory_space=pltpu.HBM)
    free = pl.BlockSpec(memory_space=pl.ANY)
    dma = pltpu.SemaphoreType.DMA
    packed = rows * chips + 2 * rank
    part_a, part_b, top, rest, pack = pl.pallas_call(
        functools.partial(front_kernel, factor),
        out_shape=(
            shape((rank, width_k), BF16),
            shape((rank, width_k), BF16),
            shape((rank, tokens), BF16),
            shape((rank, tokens), BF16),
            pltpu.HBM((tokens, packed), BF16),
        ),
        in_specs=[hbm, hbm, hbm],
        out_specs=(vmem,) * 4 + (hbm,),
        scratch_shapes=[
            pltpu.SMEM((2,), jnp.int32),
            pltpu.VMEM((tokens, width_k), BF16),
            pltpu.VMEM((tokens, packed), BF16),
            dma((4,)),
            dma((chips,)),
        ],
        cost_estimate=cost(4 * rank * width_k * tokens, 4 * rank * width_k + 2 * tokens * width_k),
        compiler_params=limit(12),
        name="front",
    )(held_key, held_grads, held)
    got = lax.ppermute(pack, "fsdp", swap)

    def whole(a, b):
        return pl.BlockSpec((a, b), lambda i, *_: (0, 0))

    partial = pl.pallas_call(
        partial_kernel,
        out_shape=pltpu.HBM((chips, rank, rows), BF16),
        in_specs=[hbm, free, vmem, vmem],
        out_specs=free,
        scratch_shapes=[
            pltpu.VMEM((chips, 2 * tokens, rows), BF16),
            pltpu.VMEM((tokens, 2 * rank), BF16),
            pltpu.VMEM((2 * rank, 2 * tokens), BF16),
            pltpu.VMEM((chips, rank, rows), BF16),
            dma((chips,)),
            dma((chips,)),
            dma((chips,)),
            dma,
        ],
        cost_estimate=cost(8 * rank * tokens * width // 2, 2 * tokens * width + 2 * rank * rows * chips),
        compiler_params=limit(16),
        name="partial",
    )(held, got, top, rest)

    landed = lax.all_to_all(partial, "fsdp", 0, 0, tiled=True, axis_index_groups=same_core)

    side_a, side_b, _ = lax.optimization_barrier((part_a, part_b, partial))
    tile = 128
    local_term, base_momentum, base_anchor = pl.pallas_call(
        functools.partial(side_kernel, unit),
        out_shape=(pltpu.HBM((rank, rows), F32), shape((rows, rank), F32), shape((rows, width_k), F32)),
        grid=(rows // tile,),
        in_specs=[
            pl.BlockSpec((tile, width_k), lambda i: (i, 0)),
            pl.BlockSpec((tile, width_k), lambda i: (i, 0)),
            pl.BlockSpec((tile, rank), lambda i: (i, 0)),
            whole(rank, width_k),
            whole(rank, width_k),
        ],
        out_specs=(
            pl.BlockSpec((rank, tile), lambda i: (0, i)),
            pl.BlockSpec((tile, rank), lambda i: (i, 0)),
            pl.BlockSpec((tile, width_k), lambda i: (i, 0)),
        ),
        cost_estimate=cost(16 * rank * rows * width_k, 10 * rows * width_k + 12 * rows * rank),
        compiler_params=limit(16),
        name="side",
    )(local, anchor, momentum, side_a, side_b)

    mine = pl.pallas_call(
        functools.partial(sum_kernel, 1.0 / replicas),
        out_shape=shape((rank, rows), BF16),
        in_specs=[free, hbm],
        out_specs=vmem,
        scratch_shapes=[pltpu.VMEM((chips, rank, rows), BF16), pltpu.VMEM((rank, rows), F32), dma, dma((4,))],
        cost_estimate=cost(chips * rank * rows, 2 * (chips + 3) * rank * rows),
        compiler_params=limit(12),
        name="gather_sum",
    )(landed, pltpu.with_memory_space_constraint(local_term, pltpu.HBM))
    pieces = lax.all_to_all(mine.reshape(8, rank // 8, rows), "replica", 0, 0, tiled=True, axis_index_groups=near)
    piece = total(pieces)
    sixths = lax.all_to_all(jnp.broadcast_to(piece[None], (6,) + piece.shape), "replica", 0, 0, tiled=True, axis_index_groups=far)
    piece = total(sixths)
    mean = lax.all_to_all(jnp.broadcast_to(piece[None], (8,) + piece.shape), "replica", 0, 0, tiled=True, axis_index_groups=near)

    new_anchor, new_momentum = pl.pallas_call(
        functools.partial(last_kernel, unit),
        out_shape=(pltpu.HBM((rows, width_k), F32), shape((rows, rank), F32)),
        in_specs=[vmem] * 5,
        out_specs=(hbm, vmem),
        scratch_shapes=[pltpu.VMEM((rows // tile, tile, width_k), F32), dma((rows // tile,))],
        cost_estimate=cost(4 * rank * rows * width_k, 8 * rows * width_k + 10 * rows * rank),
        compiler_params=limit(16),
        name="last",
    )(mean.reshape(rank, rows), base_momentum, base_anchor, part_a, part_b)
    return (new_anchor, new_momentum)


def solution(mesh):
    placed = (
        P("replica", "fsdp", None),
        P("replica", "fsdp", None),
        P("replica", "fsdp", None),
        P("fsdp", None),
        P("fsdp", None),
        P(),
    )
    return jax.shard_map(
        on_device,
        mesh=mesh,
        in_specs=placed,
        out_specs=(P("fsdp", None), P("fsdp", None)),
        check_vma=False,
    )
```

```python
import functools

import jax
import jax.numpy as jnp
from jax import lax
from jax.experimental import pallas as pl
from jax.experimental.pallas import tpu as pltpu
from jax.sharding import PartitionSpec as P

F32 = jnp.float32
BF16 = jnp.bfloat16
NN = (((1,), (0,)), ((), ()))
NT = (((1,), (1,)), ((), ()))


def mm(a, b, dims=NN):
    return lax.dot_general(a, b, dims, preferred_element_type=F32)


def split(x):
    top = x.astype(BF16)
    return top, (x - top.astype(F32)).astype(BF16)


def cost(flops, bytes_accessed):
    return pl.CostEstimate(flops=flops, bytes_accessed=bytes_accessed, transcendentals=0)


def front_kernel(factor, key_hbm, grads_hbm, acts_hbm, a_ref, b_ref, top_ref, rest_ref, own_ref, key_ref, grads_ref, sems, own_sems):
    key_copy = pltpu.make_async_copy(key_hbm, key_ref, sems.at[0])
    grads_copy = pltpu.make_async_copy(grads_hbm, grads_ref, sems.at[1])
    key_copy.start()
    grads_copy.start()
    rank, width_k = a_ref.shape
    chips = own_sems.shape[0]
    rows = own_ref.shape[1] // chips
    core = lax.rem(lax.axis_index("fsdp"), 2)
    loads = []
    for i in range(chips):
        columns = pl.ds(pl.multiple_of((2 * i + core) * rows, rows), rows)
        load = pltpu.make_async_copy(acts_hbm.at[:, columns], own_ref.at[:, pl.ds(i * rows, rows)], own_sems.at[i])
        load.start()
        loads.append(load)
    step = 256
    r_index = lax.broadcasted_iota(jnp.int32, (rank, step), 0) * 374761393
    k_index = lax.broadcasted_iota(jnp.int32, (rank, step), 1) * 668265261
    base = r_index + k_index
    key_copy.wait()
    start = key_ref[0] + key_ref[1] * 1103515245
    for k in range(0, width_k, step):
        shift = (k * 668265261 + 2**31) % 2**32 - 2**31
        hashed = base + (start + jnp.int32(shift))
        hashed = jnp.bitwise_xor(hashed, lax.shift_right_logical(hashed, jnp.int32(15)))
        hashed = hashed * 739982445
        hashed = jnp.bitwise_xor(hashed, lax.shift_right_logical(hashed, jnp.int32(12)))
        hashed = hashed * 695938361
        hashed = jnp.bitwise_xor(hashed, lax.shift_right_logical(hashed, jnp.int32(15)))
        high = jnp.bitwise_and(lax.shift_right_logical(hashed, jnp.int32(16)), 255).astype(F32)
        low = jnp.bitwise_and(lax.shift_right_logical(hashed, jnp.int32(8)), 255).astype(F32)
        a_ref[:, k : k + step] = ((high - 127.5) * 256.0).astype(BF16)
        b_ref[:, k : k + step] = (low - 127.5).astype(BF16)
    grads_copy.wait()
    grads = grads_ref[...]
    top_ref[...], rest_ref[...] = split(factor * (mm(a_ref[...], grads, NT) + mm(b_ref[...], grads, NT)))
    for load in loads:
        load.wait()


def partial_kernel(factor, own_ref, got_ref, gg_ref, a_ref, b_ref, top_ref, rest_ref, out_hbm, tops, sums, out_sems):
    chips, rank, rows = sums.shape
    tokens = own_ref.shape[0]
    core = lax.rem(lax.axis_index("fsdp"), 2)
    both = mm(jnp.concatenate([a_ref[...], b_ref[...]], axis=0), gg_ref[...], NT)
    top, rest = split(factor * (both[:rank] + both[rank:]))
    tops[:rank, :tokens] = top_ref[...]
    tops[:rank, tokens:] = top
    tops[rank:, :tokens] = rest_ref[...]
    tops[rank:, tokens:] = rest
    stores = []
    for i in range(chips):
        columns = pl.ds(pl.multiple_of((2 * i + core) * rows, rows), rows)
        acts = jnp.concatenate([own_ref[:, i * rows : (i + 1) * rows], got_ref[:, columns]], axis=0)
        product = mm(tops[...], acts)
        sums[i] = (product[:rank] + product[rank:]).astype(BF16)
        store = pltpu.make_async_copy(sums.at[i], out_hbm.at[i], out_sems.at[i])
        store.start()
        stores.append(store)
    for store in stores:
        store.wait()


def sum_kernel(portion, landed_ref, local_hbm, out_ref, local_ref, added_ref, local_sem):
    chips, rank, rows = landed_ref.shape
    local_copy = pltpu.make_async_copy(local_hbm, local_ref, local_sem)
    local_copy.start()
    step = 64
    for p in range(0, rank, step):
        span = pl.ds(p, step)
        added = landed_ref[0, span].astype(F32)
        for i in range(1, chips):
            added += landed_ref[i, span].astype(F32)
        added_ref[span] = added
    local_copy.wait()
    out_ref[...] = ((added_ref[...] - local_ref[...]) * portion).astype(BF16)


def side_kernel(unit, local_ref, anchor_ref, momentum_ref, a_ref, b_ref, local_term_ref, base_momentum_ref, base_anchor_ref):
    part_a, part_b = a_ref[...], b_ref[...]
    local = local_ref[...]
    local_term_ref[...] = unit * (mm(part_a, local, NT) + mm(part_b, local, NT))
    anchor = anchor_ref[...]
    top, rest = split(anchor)
    anchor_term = unit * (mm(top, part_a, NT) + mm(top, part_b, NT) + mm(rest, part_a, NT))
    base = 0.9 * momentum_ref[...] + anchor_term
    base_momentum_ref[...] = base
    top, rest = split(anchor_term + 0.9 * base)
    base_anchor_ref[...] = anchor - (0.7 * unit) * (mm(top, part_a) + mm(top, part_b) + mm(rest, part_a))


def last_kernel(unit, mean_ref, base_momentum_ref, base_anchor_ref, a_ref, b_ref, new_anchor_hbm, new_momentum_ref, outs, sems):
    tile = outs.shape[1]
    stores = []
    for i in range(outs.shape[0]):
        span = pl.ds(i * tile, tile)
        mean = mean_ref[:, span].astype(F32).T
        new_momentum_ref[span] = base_momentum_ref[span] + mean
        narrow = mean.astype(BF16)
        product = mm(narrow, a_ref[...]) + mm(narrow, b_ref[...])
        outs[i] = base_anchor_ref[span] - (0.7 * 1.9 * unit) * product
        store = pltpu.make_async_copy(outs.at[i], new_anchor_hbm.at[span], sems.at[i])
        store.start()
        stores.append(store)
    for store in stores:
        store.wait()


def limit(mib):
    return pltpu.CompilerParams(vmem_limit_bytes=mib << 20)


def total(x):
    return lax.reduce_precision(jnp.sum(x.astype(F32), axis=0), 8, 7).astype(BF16)


def groups(z_of, y_of):
    return [[z * 4 + y for z in zs for y in ys] for zs in z_of for ys in y_of]


def on_device(activations, grad_out, local_weight, anchor, momentum, projection_key):
    inputs, grads, local = activations[0], grad_out[0], local_weight[0]
    tokens, width = inputs.shape
    width_k, rank = grads.shape[1], momentum.shape[1]
    rows = anchor.shape[0]
    replicas, shards = lax.axis_size("replica"), lax.axis_size("fsdp")
    unit = (12.0 / float(rank)) ** 0.5 / 65536.0
    factor = unit * float(tokens * shards) ** (-0.5)
    chips = shards // 2
    swap = [(i, i ^ 1) for i in range(shards)]
    same_core = [[2 * i + c for i in range(chips)] for c in range(2)]
    near = groups([range(h, h + 4) for h in range(0, 12, 4)], [[0, 1], [3, 2]])
    far = groups([range(l, 12, 4) for l in range(4)], [[0, 3], [1, 2]])
    shape = jax.ShapeDtypeStruct

    held = pltpu.with_memory_space_constraint(inputs, pltpu.HBM)
    held_grads = pltpu.with_memory_space_constraint(grads, pltpu.HBM)
    held_key = pltpu.with_memory_space_constraint(projection_key, pltpu.HBM)
    got = lax.ppermute(inputs, "fsdp", swap)
    got_grads = lax.ppermute(grads, "fsdp", swap)

    vmem = pl.BlockSpec(memory_space=pltpu.VMEM)
    hbm = pl.BlockSpec(memory_space=pltpu.HBM)
    dma = pltpu.SemaphoreType.DMA
    part_a, part_b, top, rest, own = pl.pallas_call(
        functools.partial(front_kernel, factor),
        out_shape=(
            shape((rank, width_k), BF16),
            shape((rank, width_k), BF16),
            shape((rank, tokens), BF16),
            shape((rank, tokens), BF16),
            shape((tokens, rows * chips), BF16),
        ),
        in_specs=[hbm] * 3,
        out_specs=(vmem,) * 5,
        scratch_shapes=[pltpu.SMEM((2,), jnp.int32), pltpu.VMEM((tokens, width_k), BF16), dma((2,)), dma((chips,))],
        cost_estimate=cost(4 * rank * width_k * tokens, 4 * rank * width_k + 2 * tokens * width_k),
        compiler_params=limit(12),
        name="front",
    )(held_key, held_grads, held)

    def whole(a, b):
        return pl.BlockSpec((a, b), lambda i, *_: (0, 0))

    partial = pl.pallas_call(
        functools.partial(partial_kernel, factor),
        out_shape=pltpu.HBM((chips, rank, rows), BF16),
        in_specs=[vmem] * 7,
        out_specs=hbm,
        scratch_shapes=[
            pltpu.VMEM((2 * rank, 2 * tokens), BF16),
            pltpu.VMEM((chips, rank, rows), BF16),
            dma((chips,)),
        ],
        cost_estimate=cost(8 * rank * tokens * width // 2, 2 * tokens * width + 2 * rank * rows * chips),
        compiler_params=limit(16),
        name="partial",
    )(own, got, got_grads, part_a, part_b, top, rest)

    landed = lax.all_to_all(partial, "fsdp", 0, 0, tiled=True, axis_index_groups=same_core)

    side_a, side_b, _ = lax.optimization_barrier((part_a, part_b, partial))
    tile = 128
    local_term, base_momentum, base_anchor = pl.pallas_call(
        functools.partial(side_kernel, unit),
        out_shape=(pltpu.HBM((rank, rows), F32), shape((rows, rank), F32), shape((rows, width_k), F32)),
        grid=(rows // tile,),
        in_specs=[
            pl.BlockSpec((tile, width_k), lambda i: (i, 0)),
            pl.BlockSpec((tile, width_k), lambda i: (i, 0)),
            pl.BlockSpec((tile, rank), lambda i: (i, 0)),
            whole(rank, width_k),
            whole(rank, width_k),
        ],
        out_specs=(
            pl.BlockSpec((rank, tile), lambda i: (0, i)),
            pl.BlockSpec((tile, rank), lambda i: (i, 0)),
            pl.BlockSpec((tile, width_k), lambda i: (i, 0)),
        ),
        cost_estimate=cost(16 * rank * rows * width_k, 10 * rows * width_k + 12 * rows * rank),
        compiler_params=limit(16),
        name="side",
    )(local, anchor, momentum, side_a, side_b)

    mine = pl.pallas_call(
        functools.partial(sum_kernel, 1.0 / replicas),
        out_shape=shape((rank, rows), BF16),
        in_specs=[vmem, hbm],
        out_specs=vmem,
        scratch_shapes=[pltpu.VMEM((rank, rows), F32), pltpu.VMEM((rank, rows), F32), dma],
        cost_estimate=cost(chips * rank * rows, 2 * (chips + 3) * rank * rows),
        compiler_params=limit(12),
        name="gather_sum",
    )(landed, pltpu.with_memory_space_constraint(local_term, pltpu.HBM))
    pieces = lax.all_to_all(mine.reshape(8, rank // 8, rows), "replica", 0, 0, tiled=True, axis_index_groups=near)
    piece = total(pieces)
    sixths = lax.all_to_all(jnp.broadcast_to(piece[None], (6,) + piece.shape), "replica", 0, 0, tiled=True, axis_index_groups=far)
    piece = total(sixths)
    mean = lax.all_to_all(jnp.broadcast_to(piece[None], (8,) + piece.shape), "replica", 0, 0, tiled=True, axis_index_groups=near)

    new_anchor, new_momentum = pl.pallas_call(
        functools.partial(last_kernel, unit),
        out_shape=(pltpu.HBM((rows, width_k), F32), shape((rows, rank), F32)),
        in_specs=[vmem] * 5,
        out_specs=(hbm, vmem),
        scratch_shapes=[pltpu.VMEM((rows // tile, tile, width_k), F32), dma((rows // tile,))],
        cost_estimate=cost(4 * rank * rows * width_k, 8 * rows * width_k + 10 * rows * rank),
        compiler_params=limit(16),
        name="last",
    )(mean.reshape(rank, rows), base_momentum, base_anchor, part_a, part_b)
    return (new_anchor, new_momentum)


def solution(mesh):
    placed = (
        P("replica", "fsdp", None),
        P("replica", "fsdp", None),
        P("replica", "fsdp", None),
        P("fsdp", None),
        P("fsdp", None),
        P(),
    )
    return jax.shard_map(
        on_device,
        mesh=mesh,
        in_specs=placed,
        out_specs=(P("fsdp", None), P("fsdp", None)),
        check_vma=False,
    )
```
